32 devices in a mesh: dp: 4 (over z), ctx: 8 (over y, x, core).
Axes of the slice: x: 2, y: 2, z: 4, core: 2. Of those that a mesh axis runs over, the one named last changes fastest.
Arguments:
- hidden: bfloat16 [4, 1024, 4096], P('dp', 'ctx'), may hold values from -6 to 6
- query_in: bfloat16 [4, 1024, 2048], P('dp', 'ctx'), may hold values from -6 to 6
- key_in: bfloat16 [4, 1024, 2048], P('dp', 'ctx'), may hold values from -6 to 6
- value_in: bfloat16 [4, 1024, 2048], P('dp', 'ctx'), may hold values from -6 to 6
- w_proj: bfloat16 [4096, 32], P('dp'), may hold values from -0.09375 to 0.09375
- decay_rate: float32 [16], replicated, may hold values from 9.765625e-05 to 0.03
- dt_bias: float32 [16], replicated, may hold values from -1 to 1
- beta_bias: float32 [16], replicated, may hold values from -6 to 1
- norm_gain: float32 [128], replicated, may hold values from 0.25 to 1.75
- doc_starts: int32 [4, 4], P('dp'), may hold values from 0 to 15, as said below
- grad_out: bfloat16 [4, 1024, 2048], P('dp', 'ctx'), may hold values from -6 to 6
Outputs:
- normed_out: bfloat16 [4, 1024, 2048], P('dp', 'ctx')
- grad_query: bfloat16 [4, 1024, 2048], P('dp', 'ctx')
- grad_key: bfloat16 [4, 1024, 2048], P('dp', 'ctx')
- grad_value: bfloat16 [4, 1024, 2048], P('dp', 'ctx')
- grad_hidden: bfloat16 [4, 1024, 4096], P('dp', 'ctx')
- grad_weight: float32 [4096, 32], P('dp')
The draws below stay inside these ranges and needn't reach their ends.
Inputs may be any that keep to these rules, and one draw needn't show every extreme that they name: `doc_starts`: row s lists the first blocks (64 tokens each) of the 4 documents of sequence s: 0 first, then rising strictly.
All inputs are finite; a program needn't handle non-finite values.
Results may differ from the reference program's by a relative error of at most 0.0049.
Values may be sent and summed in bfloat16 or wider, within the bound.
No kernel may reach another device: no remote copies, remote signals or barrier semaphores. Data moves between devices by JAX's collectives and lax.ppermute only.
A program may use at most 384 MiB of HBM per device.

```python
import math
import jax
import jax.numpy as jnp
from jax import lax

D = 4096
H = 16
DK = 128
DV = 128
BLK = 64
NDOC = 4
SEQS = 4
SEQLEN = 1024
NBLK = 16
HK = 2048
HV = 2048


def draw_doc_starts(key, part):
    sequence_keys = jax.random.split(key, SEQS)

    def one_row(row_key):
        picked = jax.random.permutation(row_key, NBLK - 1)[:NDOC - 1] + 1
        return jnp.concatenate([jnp.zeros((1,), jnp.int32), jnp.sort(picked).astype(jnp.int32)])
    return jax.vmap(one_row)(sequence_keys)


def level_of(rng, dims, cuts, smallest, top_value):
    level, own = 1.0, jax.random.fold_in(rng, 6)
    for dim, shards_of in cuts:
        heights = jnp.exp(jax.random.uniform(jax.random.fold_in(own, dim), (shards_of,), jnp.float32, smallest / len(cuts), top_value / len(cuts)))
        level = level * jnp.repeat(heights, dims[dim] // shards_of).reshape([-1 if axis == dim else 1 for axis in range(len(dims))])
    return level


def normal_values(key, extent, scale, most, cuts=(), kind=jnp.bfloat16):
    entries = jax.random.normal(key, extent, jnp.float32) * scale
    if len(cuts) > 0:
        entries = level_of(key, extent, cuts, -0.22, 0.18) * entries
    return jnp.clip(entries, min=-most, max=most).astype(kind)


def setup_inputs(seed: int = 0) -> dict:
    seeds = jax.random.split(jax.random.key(seed), 12)
    hidden = normal_values(seeds[0], (SEQS, SEQLEN, D), 1.0, 6.0, ((0, 4), (1, 8)))
    query_in = normal_values(seeds[1], (SEQS, SEQLEN, HK), 1.0, 6.0, ((0, 4), (1, 8)))
    key_in = normal_values(seeds[2], (SEQS, SEQLEN, HK), 1.0, 6.0, ((0, 4), (1, 8)))
    value_in = normal_values(seeds[3], (SEQS, SEQLEN, HV), 1.0, 6.0, ((0, 4), (1, 8)))
    w_proj = normal_values(seeds[4], (D, 2 * H), D ** -0.5, 0.09375, ((0, 4),))
    decay_rate = jnp.clip(jnp.exp(jax.random.uniform(seeds[5], (H,), jnp.float32, math.log(9.765625145519152e-05), math.log(0.03))), 9.765625145519152e-05, 0.03)
    dt_bias = jnp.clip(jax.random.uniform(seeds[6], (H,), jnp.float32, -1.0, 1.0), -1.0, 1.0)
    beta_bias = jnp.clip(jax.random.uniform(seeds[7], (H,), jnp.float32, -6.0, 1.0), -6.0, 1.0)
    norm_gain = jnp.clip(1.0 + 0.15 * jax.random.normal(seeds[8], (DV,), jnp.float32), 0.25, 1.75)
    doc_starts = draw_doc_starts(jax.random.fold_in(seeds[11], 71), 0)
    grad_out = normal_values(seeds[10], (SEQS, SEQLEN, HV), 1.0, 6.0, ((0, 4), (1, 8)))
    return dict(hidden=hidden, query_in=query_in, key_in=key_in, value_in=value_in, w_proj=w_proj, decay_rate=decay_rate, dt_bias=dt_bias, beta_bias=beta_bias, norm_gain=norm_gain, doc_starts=doc_starts, grad_out=grad_out)


def unit_rows(matrix):
    return matrix * lax.rsqrt(lax.optimization_barrier(jnp.sum(matrix * matrix, axis=-1, keepdims=True)) + 1e-06)

def rms_scaled(values, norm_gain):
    return values * lax.rsqrt(lax.optimization_barrier(jnp.mean(values * values, axis=-1, keepdims=True)) + 1e-05) * norm_gain

def gate_terms(logit_rows, decay_rate, dt_bias, beta_bias):
    head_count = decay_rate.shape[0]
    log_decay = -decay_rate * jax.nn.softplus(logit_rows[:, :head_count] + dt_bias)
    beta_rows = jax.nn.sigmoid(logit_rows[:, head_count:] + beta_bias)
    return (log_decay, beta_rows)

def keep_blocks(starts, first_block, block_count):
    block_ids = first_block + jnp.arange(block_count, dtype=jnp.int32)
    starting = jnp.any(starts[:, None] == block_ids[None, :], axis=0) & (block_ids > 0)
    return jnp.where(starting, 0.0, 1.0).astype(jnp.float32)

def blockwise(query_rows, key_rows, value_rows, log_decay, beta_rows, keep_rows, state_first):
    head_count = log_decay.shape[-1]
    row_count = query_rows.shape[0]
    blocks = row_count // BLK
    key_dim = state_first.shape[1]
    state_width = state_first.shape[2]
    val_dim = value_rows.shape[1] // head_count
    maximum_precision = lax.Precision.HIGHEST

    def advance(state_now, pieces):
        query_piece, key_piece, value_piece, decay_piece, beta_piece, keep_piece = pieces
        length = query_piece.shape[0]
        query_unit = unit_rows(query_piece.astype(jnp.float32).reshape(length, head_count, key_dim))
        key_unit = unit_rows(key_piece.astype(jnp.float32).reshape(length, head_count, key_dim))
        value_heads = value_piece.astype(jnp.float32).reshape(length, head_count, val_dim)
        state_now = state_now * keep_piece
        cumulative = jnp.cumsum(decay_piece, axis=0).T
        spread = cumulative[:, :, None] - cumulative[:, None, :]
        row_ids = lax.broadcasted_iota(jnp.int32, (length, length), 0)
        col_ids = lax.broadcasted_iota(jnp.int32, (length, length), 1)
        lower_mask = row_ids >= col_ids
        strict_mask = row_ids > col_ids
        decay_ratio = jnp.where(lower_mask, jnp.exp(jnp.where(lower_mask, spread, 0.0)), 0.0)
        key_gram = jnp.einsum('ihd,jhd->hij', key_unit, key_unit, precision=maximum_precision)
        query_gram = jnp.einsum('ihd,jhd->hij', query_unit, key_unit, precision=maximum_precision)
        beta_heads = beta_piece.T
        lower_matrix = jnp.where(strict_mask, beta_heads[:, :, None] * key_gram * decay_ratio, 0.0)
        decay_now = jnp.exp(cumulative)
        right_side = jnp.concatenate([beta_heads[:, :, None] * value_heads.transpose(1, 0, 2), (beta_heads * decay_now)[:, :, None] * key_unit.transpose(1, 0, 2)], axis=-1)
        solved = jax.scipy.linalg.solve_triangular(lower_matrix, right_side, lower=True, unit_diagonal=True)
        new_values = solved[..., :val_dim]
        key_weights = solved[..., val_dim:]
        if state_width > val_dim:
            new_values = jnp.concatenate([new_values, jnp.zeros((head_count, length, state_width - val_dim), jnp.float32)], axis=-1)
        corrected = new_values - jnp.einsum('hcd,hdw->hcw', key_weights, state_now, precision=maximum_precision)
        from_state = jnp.einsum('chd,hdw->hcw', query_unit, state_now, precision=maximum_precision)
        output_piece = decay_now[:, :, None] * from_state + jnp.einsum('hij,hjw->hiw', query_gram * decay_ratio, corrected, precision=maximum_precision)
        tail_decay = jnp.exp(cumulative[:, -1:] - cumulative)
        next_state = jnp.exp(cumulative[:, -1])[:, None, None] * state_now + jnp.einsum('chd,hcw->hdw', key_unit, tail_decay[:, :, None] * corrected, precision=maximum_precision)
        return (next_state, output_piece.transpose(1, 0, 2))
    final_state, outputs = lax.scan(advance, state_first, (query_rows.reshape(blocks, BLK, -1), key_rows.reshape(blocks, BLK, -1), value_rows.reshape(blocks, BLK, -1), log_decay.reshape(blocks, BLK, head_count), beta_rows.reshape(blocks, BLK, head_count), keep_rows))
    return (outputs.reshape(row_count, head_count, state_width), final_state)

def reference(hidden, query_in, key_in, value_in, w_proj, decay_rate, dt_bias, beta_bias, norm_gain, doc_starts, grad_out):
    flat_hidden = hidden.reshape(SEQS * SEQLEN, D)
    logits_all = jnp.dot(flat_hidden.astype(jnp.float32), w_proj.astype(jnp.float32), preferred_element_type=jnp.float32).reshape(SEQS, SEQLEN, 2 * H)

    def one_sequence(pieces):
        query_rows, key_rows, value_rows, logit_rows, starts, cotangent = pieces
        keep_rows = keep_blocks(starts, 0, NBLK)

        def forward(query_part, key_part, value_part, logit_part):
            decay_part, beta_part = gate_terms(logit_part, decay_rate, dt_bias, beta_bias)
            outputs, final_state = blockwise(query_part, key_part, value_part, decay_part, beta_part, keep_rows, jnp.zeros((H, DK, DV), jnp.float32))
            return rms_scaled(outputs, norm_gain)
        normed_rows, pull_back = jax.vjp(forward, query_rows, key_rows, value_rows, logit_rows)
        gradients = pull_back(cotangent.astype(jnp.float32).reshape(SEQLEN, H, DV))
        return (normed_rows.reshape(SEQLEN, HV).astype(jnp.bfloat16), gradients[0], gradients[1], gradients[2], gradients[3])
    normed_all, grad_query, grad_key, grad_value, grad_logits = lax.map(one_sequence, (query_in, key_in, value_in, logits_all, doc_starts, grad_out))
    rounded = grad_logits.astype(jnp.bfloat16).reshape(SEQS * SEQLEN, 2 * H)
    grad_hidden = jnp.dot(rounded.astype(jnp.float32), w_proj.T.astype(jnp.float32), preferred_element_type=jnp.float32).astype(jnp.bfloat16)
    grad_weight = jnp.dot(flat_hidden.T.astype(jnp.float32), rounded.astype(jnp.float32), preferred_element_type=jnp.float32)
    return (normed_all, grad_query, grad_key, grad_value, grad_hidden.reshape(SEQS, SEQLEN, D), grad_weight)
```

```python
import functools

import jax
import jax.numpy as jnp
from jax import lax
from jax.experimental import pallas as pl
from jax.experimental.pallas import tpu as pltpu
from jax.sharding import PartitionSpec as P

BLK = 64


def entering(array, axis, combine, identity, reverse):
    devices, position = (lax.axis_size(axis), lax.axis_index(axis))
    everything = jax.tree.map(lambda part: lax.all_gather(part, axis), array)
    start = jax.tree.map(
        lambda part, zero: jnp.broadcast_to(jnp.asarray(zero, part.dtype), part.shape),
        array,
        identity,
    )

    def step(k, before):
        at = devices - 1 - k if reverse else k
        reached = at > position if reverse else at < position
        new = combine(before, jax.tree.map(lambda part: part[at], everything))
        return jax.tree.map(lambda a, b: jnp.where(reached, a, b), new, before)

    return lax.fori_loop(0, devices, step, start)


def unit_rows(matrix):
    return matrix * lax.rsqrt(jnp.sum(matrix * matrix, axis=-1, keepdims=True) + 1e-06)


def rms_scaled(values, norm_gain):
    return values * lax.rsqrt(jnp.mean(values * values, axis=-1, keepdims=True) + 1e-05) * norm_gain


def gate_terms(logit_rows, decay_rate, dt_bias, beta_bias):
    head_count = decay_rate.shape[0]
    log_decay = -decay_rate * jax.nn.softplus(logit_rows[:, :head_count] + dt_bias)
    beta_rows = jax.nn.sigmoid(logit_rows[:, head_count:] + beta_bias)
    return (log_decay, beta_rows)


def keep_blocks(starts, first_block, block_count):
    block_ids = first_block + jnp.arange(block_count, dtype=jnp.int32)
    starting = jnp.any(starts[:, None] == block_ids[None, :], axis=0) & (block_ids > 0)
    return jnp.where(starting, 0.0, 1.0).astype(jnp.float32)


def unit_lower_inverse(lower_matrix, length):
    maximum_precision = lax.Precision.HIGHEST
    identity_block = jnp.eye(length, dtype=jnp.float32)
    power_term = -lower_matrix
    inverse = identity_block + power_term
    squarings = max(1, (length - 1).bit_length())
    for level in range(squarings - 1):
        power_term = jnp.einsum("hij,hjk->hik", power_term, power_term, precision=maximum_precision)
        inverse = jnp.einsum(
            "hij,hjk->hik", inverse, identity_block + power_term, precision=maximum_precision
        )
    return inverse


def blockwise(query_rows, key_rows, value_rows, log_decay, beta_rows, keep_rows, state_first):
    head_count = log_decay.shape[-1]
    row_count = query_rows.shape[0]
    blocks = row_count // BLK
    key_dim = state_first.shape[1]
    state_width = state_first.shape[2]
    val_dim = value_rows.shape[1] // head_count
    maximum_precision = lax.Precision.HIGHEST

    def advance(state_now, pieces):
        query_piece, key_piece, value_piece, decay_piece, beta_piece, keep_piece = pieces
        length = query_piece.shape[0]
        query_unit = unit_rows(query_piece.astype(jnp.float32).reshape(length, head_count, key_dim))
        key_unit = unit_rows(key_piece.astype(jnp.float32).reshape(length, head_count, key_dim))
        value_heads = value_piece.astype(jnp.float32).reshape(length, head_count, val_dim)
        state_now = state_now * keep_piece
        cumulative = jnp.cumsum(decay_piece, axis=0).T
        spread = cumulative[:, :, None] - cumulative[:, None, :]
        row_ids = lax.broadcasted_iota(jnp.int32, (length, length), 0)
        col_ids = lax.broadcasted_iota(jnp.int32, (length, length), 1)
        lower_mask = row_ids >= col_ids
        strict_mask = row_ids > col_ids
        decay_ratio = jnp.where(lower_mask, jnp.exp(jnp.where(lower_mask, spread, 0.0)), 0.0)
        key_gram = jnp.einsum("ihd,jhd->hij", key_unit, key_unit, precision=maximum_precision)
        query_gram = jnp.einsum("ihd,jhd->hij", query_unit, key_unit, precision=maximum_precision)
        beta_heads = beta_piece.T
        lower_matrix = jnp.where(strict_mask, beta_heads[:, :, None] * key_gram * decay_ratio, 0.0)
        decay_now = jnp.exp(cumulative)
        right_side = jnp.concatenate(
            [
                beta_heads[:, :, None] * value_heads.transpose(1, 0, 2),
                (beta_heads * decay_now)[:, :, None] * key_unit.transpose(1, 0, 2),
            ],
            axis=-1,
        )
        inverse = unit_lower_inverse(lower_matrix, length)
        solved = jnp.einsum("hij,hjw->hiw", inverse, right_side, precision=maximum_precision)
        new_values = solved[..., :val_dim]
        key_weights = solved[..., val_dim:]
        new_values = jnp.concatenate(
            [new_values, jnp.zeros((head_count, length, state_width - val_dim), jnp.float32)],
            axis=-1,
        )
        corrected = new_values - jnp.einsum(
            "hcd,hdw->hcw", key_weights, state_now, precision=maximum_precision
        )
        from_state = jnp.einsum("chd,hdw->hcw", query_unit, state_now, precision=maximum_precision)
        output_piece = decay_now[:, :, None] * from_state + jnp.einsum(
            "hij,hjw->hiw", query_gram * decay_ratio, corrected, precision=maximum_precision
        )
        tail_decay = jnp.exp(cumulative[:, -1:] - cumulative)
        next_state = jnp.exp(cumulative[:, -1])[:, None, None] * state_now + jnp.einsum(
            "chd,hcw->hdw",
            key_unit,
            tail_decay[:, :, None] * corrected,
            precision=maximum_precision,
        )
        return (next_state, output_piece.transpose(1, 0, 2))

    final_state, outputs = lax.scan(
        advance,
        state_first,
        (
            query_rows.reshape(blocks, BLK, -1),
            key_rows.reshape(blocks, BLK, -1),
            value_rows.reshape(blocks, BLK, -1),
            log_decay.reshape(blocks, BLK, head_count),
            beta_rows.reshape(blocks, BLK, head_count),
            keep_rows,
        ),
    )
    return (outputs.reshape(row_count, head_count, state_width), final_state)


def combine_pairs(earlier_pair, later_pair):
    maximum_precision = lax.Precision.HIGHEST
    joined_map = jnp.einsum(
        "hij,hjk->hik", later_pair[0], earlier_pair[0], precision=maximum_precision
    )
    joined_offset = (
        jnp.einsum("hij,hjk->hik", later_pair[0], earlier_pair[1], precision=maximum_precision)
        + later_pair[1]
    )
    return (joined_map, joined_offset)


def shards(
    hidden,
    query_in,
    key_in,
    value_in,
    w_proj,
    decay_rate,
    dt_bias,
    beta_bias,
    norm_gain,
    doc_starts,
    grad_out,
):
    maximum_precision = lax.Precision.HIGHEST
    tokens_here = hidden[0]
    row_count = tokens_here.shape[0]
    head_count = decay_rate.shape[0]
    val_dim = norm_gain.shape[0]
    key_dim = query_in.shape[2] // head_count
    logits = jnp.dot(
        tokens_here,
        lax.all_gather(w_proj, "dp", axis=0, tiled=True),
        preferred_element_type=jnp.float32,
    )
    block_count = row_count // BLK
    keep_rows = keep_blocks(doc_starts[0], lax.axis_index("ctx") * block_count, block_count)
    identity_map = jnp.broadcast_to(
        jnp.eye(key_dim, dtype=jnp.float32), (head_count, key_dim, key_dim)
    )
    empty_state = jnp.zeros((head_count, key_dim, val_dim), jnp.float32)
    start_state = jnp.concatenate([empty_state, identity_map], axis=-1)

    def first_pass(query_rows, key_rows, value_rows, logit_rows):
        decay_part, beta_part = gate_terms(logit_rows, decay_rate, dt_bias, beta_bias)
        return blockwise(
            query_rows, key_rows, value_rows, decay_part, beta_part, keep_rows, start_state
        )

    pass_result, pull_core = jax.vjp(first_pass, query_in[0], key_in[0], value_in[0], logits)
    summary, closing = pass_result
    transfer = closing[..., val_dim:]
    offset = closing[..., :val_dim]
    state_sensitivity = summary[..., val_dim:]
    prefix = entering((transfer, offset), "ctx", combine_pairs, (identity_map, empty_state), False)
    incoming_state = prefix[1]
    mixed_rows = summary[..., :val_dim] + jnp.einsum(
        "ihd,hdl->ihl", state_sensitivity, incoming_state, precision=maximum_precision
    )
    normed_rows, pull_norm = jax.vjp(lambda values: rms_scaled(values, norm_gain), mixed_rows)
    incoming = grad_out[0].astype(jnp.float32).reshape(row_count, head_count, val_dim)
    mixed_gradient = pull_norm(incoming)[0]
    local_sensitivity = jnp.einsum(
        "idl,ids->dls", state_sensitivity, mixed_gradient, precision=maximum_precision
    )
    suffix = entering(
        (jnp.swapaxes(transfer, 1, 2), local_sensitivity),
        "ctx",
        combine_pairs,
        (identity_map, empty_state),
        True,
    )
    leaving = suffix[1]
    sensitivity_grad = jnp.einsum(
        "ihl,hdl->ihd", mixed_gradient, incoming_state, precision=maximum_precision
    )
    transfer_grad = jnp.einsum("hil,hjl->hij", leaving, incoming_state, precision=maximum_precision)
    summary_grad = jnp.concatenate([mixed_gradient, sensitivity_grad], axis=-1)
    closing_grad = jnp.concatenate([leaving, transfer_grad], axis=-1)
    grad_q, grad_k, grad_v, grad_logit = pull_core((summary_grad, closing_grad))
    rounded = grad_logit.astype(jnp.bfloat16)
    back_rows = jnp.dot(
        rounded,
        lax.all_gather(w_proj, "dp", axis=0, tiled=True).T,
        preferred_element_type=jnp.float32,
    )
    weight_term = lax.dot_general(
        tokens_here, rounded, (((0,), (0,)), ((), ())), preferred_element_type=jnp.float32
    )
    summed = lax.psum(weight_term, "ctx")
    weight_grad = lax.psum_scatter(summed, "dp", scatter_dimension=0, tiled=True)
    return (
        normed_rows.reshape(1, row_count, -1).astype(jnp.bfloat16),
        grad_q.reshape(1, row_count, -1),
        grad_k.reshape(1, row_count, -1),
        grad_v.reshape(1, row_count, -1),
        back_rows.astype(jnp.bfloat16).reshape(1, row_count, -1),
        weight_grad,
    )


def dot(a, b, ca, cb):
    return lax.dot_general(a, b, (((ca,), (cb,)), ((), ())), preferred_element_type=jnp.float32)


def halves(a):
    high = a.astype(jnp.bfloat16)
    return (high, (a - high.astype(jnp.float32)).astype(jnp.bfloat16))


def mul(a, b, ca=1, cb=0):
    ah, al = halves(a)
    bh, bl = halves(b)
    return dot(ah, bh, ca, cb) + (dot(ah, bl, ca, cb) + dot(al, bh, ca, cb))


def cast_mul(a, b, ca=1, cb=0):
    return dot(a.astype(jnp.bfloat16), b.astype(jnp.bfloat16), ca, cb)


def row_sum(a):
    return jnp.sum(a, axis=1, keepdims=True)


def flip(index, mask):
    out = index
    bit = 1
    while bit <= mask:
        if mask & bit:
            out = out + bit * (1 - 2 * ((index // bit) % 2))
        bit *= 2
    return out


def pack_kernel(place, *refs):
    arrays, outs = refs[:4], refs[4:]
    width = outs[0].shape[2]
    for mask, out in enumerate(outs):
        at = pl.multiple_of(flip(place[0], mask) * width, width)
        for which, array in enumerate(arrays):
            out[which] = array[:, pl.ds(at, width)]


def unpack_kernel(place, *refs):
    outs = refs[-4:]
    for mask, part in enumerate(refs[:-4]):
        width = part.shape[2]
        at = pl.multiple_of(flip(place[0], mask) * width, width)
        for which, out in enumerate(outs):
            out[:, pl.ds(at, width)] = part[which]


def logits_kernel(place, hidden, *refs):
    out = refs[-1]
    total = None
    for mask, part in enumerate(refs[:-1]):
        depth = part.shape[1]
        at = pl.multiple_of(flip(place[0], mask) * depth, depth)
        term = dot(part[...], hidden[:, pl.ds(at, depth)], 1, 1)
        total = term if total is None else total + term
    out[...] = total


def tail_kernel(place, hidden, grads, *refs):
    count = (len(refs) - 1) // 2
    parts, back, outs = refs[:count], refs[count], refs[count + 1 :]
    rounded = grads[...].astype(jnp.bfloat16)
    for mask in range(count):
        depth = parts[mask].shape[1]
        at = pl.multiple_of(flip(place[0], mask) * depth, depth)
        back[:, pl.ds(at, depth)] = dot(rounded, parts[mask][...], 0, 0).astype(jnp.bfloat16)
        outs[mask][...] = dot(rounded, hidden[:, pl.ds(at, depth)], 1, 0).astype(outs[mask].dtype)


def core_kernel(heads, devices, place, keep, gate_rows, gate_cols, slopes, gain, *refs):
    received, refs = refs[:devices], refs[devices:]
    sent, refs = refs[:devices], refs[devices:]
    grads, inputs, results, qs, ks, us, ws, ps, xs, gs, cs, os_, ds, states, scales, running = refs
    length = gate_rows.shape[2]
    half = length // 2
    f32 = jnp.float32
    for mask, part in enumerate(received):
        inputs[flip(place[0], mask)] = part[...]
    rows = lax.broadcasted_iota(jnp.int32, (length, length), 0)
    cols = lax.broadcasted_iota(jnp.int32, (length, length), 1)
    lower = rows >= cols
    strict = rows > cols
    same_half = (rows >= half) == (cols >= half)
    second = lax.broadcasted_iota(jnp.int32, (length, 1), 0) >= half
    unit = jnp.where(rows == cols, 1.0, 0.0).astype(f32)
    gain_row = gain[...]

    def piece(s, which, h):
        return inputs[s, which, :, h * 128 : (h + 1) * 128].astype(f32)

    def decays(s, h):
        c_col = gate_cols[s, :, h : h + 1]
        beta = gate_cols[s, :, heads + h : heads + h + 1]
        keep0, keep1 = keep[2 * s], keep[2 * s + 1]
        last = gate_cols[s, length - 1 :, h : h + 1]
        now = jnp.exp(c_col) * jnp.where(second, keep1, 1.0) * keep0
        tail = jnp.exp(last - c_col) * jnp.where(second, 1.0, keep1)
        whole = jnp.exp(last) * (keep0 * keep1)
        return beta, now, tail, whole

    def ratio(s, h):
        c_col = gate_cols[s, :, h : h + 1]
        c_row = gate_rows[s, h : h + 1, :]
        kept = jnp.where(same_half, 1.0, keep[2 * s + 1])
        return jnp.where(lower, jnp.exp(c_col - c_row), 0.0) * kept

    group = PREPARE
    def prepare(step, carry):
        items = [(step * group + d, h) for d in range(group) for h in range(heads)]
        work = []
        for s, h in items:
            query, key = piece(s, 0, h), piece(s, 1, h)
            rq = lax.rsqrt(row_sum(query * query) + 1e-06)
            rk = lax.rsqrt(row_sum(key * key) + 1e-06)
            scales[s, :, h : h + 1] = rq
            scales[s, :, heads + h : heads + h + 1] = rk
            query, key = query * rq, key * rk
            qs[s, h], ks[s, h] = query, key
            gram = mul(key, key, 1, 1)
            cross = mul(query, key, 1, 1)
            gamma = ratio(s, h)
            beta, now, tail, whole = decays(s, h)
            ps[s, h] = cross * gamma
            gram = jnp.where(strict, gram * gamma, 0.0)
            gs[s, h] = gram
            work.append([beta * gram, key, beta, now])
        inverses = [unit - jnp.where(rows // 2 == cols // 2, w[0], 0.0) for w in work]
        size = 2
        while size < length:
            joined = (rows // (2 * size) == cols // (2 * size)) & (rows // size != cols // size)
            inner = [mul(jnp.where(joined, w[0], 0.0), x) for w, x in zip(work, inverses)]
            inverses = [x - mul(x, y) for x, y in zip(inverses, inner)]
            size *= 2
        for (s, h), (_, key, beta, now), x in zip(items, work, inverses):
            xs[s, h] = x
            us[s, h] = mul(x, beta * piece(s, 2, h))
            ws[s, h] = mul(x, (beta * now) * key)
        return carry

    lax.fori_loop(0, devices // group, prepare, 0)
    running[...] = jnp.zeros_like(running)

    def forward(s, carry):
        for h in range(heads):
            beta, now, tail, whole = decays(s, h)
            state = running[h]
            states[s, h] = state
            both = mul(jnp.concatenate([ws[s, h], qs[s, h]], axis=0), state)
            corrected = us[s, h] - both[:length]
            from_state = now * both[length:]
            mixed = from_state + mul(ps[s, h], corrected)
            running[h] = whole * state + mul(ks[s, h], tail * corrected, 0, 0)
            cs[s, h], os_[s, h] = corrected, from_state
            scale = lax.rsqrt(row_sum(mixed * mixed) * (1.0 / length) + 1e-05)
            results[s, 0, :, h * 128 : (h + 1) * 128] = (mixed * scale * gain_row).astype(jnp.bfloat16)
            slope = piece(s, 3, h) * gain_row
            inner = row_sum(mixed * slope) * (1.0 / length)
            ds[s, h] = scale * (slope - mixed * (scale * scale * inner))
        return carry

    lax.fori_loop(0, devices, forward, 0)
    running[...] = jnp.zeros_like(running)
    suffix = jnp.where(lower, 1.0, 0.0).astype(f32)

    def backward(step, carry):
        s = devices - 1 - step
        columns = []
        column_rows = []
        totals = []
        for h in range(heads):
            beta, now, tail, whole = decays(s, h)
            leaving = running[h]
            state, key, query = states[s, h], ks[s, h], qs[s, h]
            grad, corrected, weights = ds[s, h], cs[s, h], ws[s, h]
            key_leaving = mul(key, leaving)
            d_corr = mul(ps[s, h], grad, 0, 0) + tail * key_leaving
            pair = jnp.concatenate([now * grad, -d_corr], axis=0)
            running[h] = whole * leaving + mul(jnp.concatenate([query, weights], axis=0), pair, 0, 0)
            through = mul(pair, state, 1, 1)
            d_query, d_weights = through[:length], through[length:]
            gamma = ratio(s, h)
            d_cross = mul(grad, corrected, 1, 1) * gamma
            second_term = mul(grad, corrected, 1, 1) * ps[s, h]
            d_query = d_query + mul(d_cross, key)
            tailed = tail * corrected
            d_key = mul(d_cross, query, 0, 0) + mul(tailed, leaving, 1, 1)
            x = xs[s, h]
            d_right = mul(x, jnp.concatenate([d_corr, d_weights], axis=1), 0, 0)
            d_right_u, d_right_w = d_right[:, :length], d_right[:, length:]
            d_lower = -mul(d_right, jnp.concatenate([us[s, h], weights], axis=1), 1, 1)
            d_lower = jnp.where(strict, d_lower, 0.0)
            first_term = d_lower * gs[s, h]
            d_gram = beta * d_lower * gamma
            d_key = d_key + mul(d_gram, key) + mul(d_gram, key, 0, 0)
            d_key = d_key + (beta * now) * d_right_w
            d_value = beta * d_right_u
            keyed = now * d_right_w * key
            moved = tailed * key_leaving
            both_terms = beta * first_term + second_term
            columns.append(row_sum(grad * os_[s, h] + beta * keyed + both_terms - moved))
            columns.append(row_sum(d_right_u * piece(s, 2, h) + keyed + first_term))
            column_rows.append(jnp.sum(both_terms, axis=0, keepdims=True))
            everything = jnp.sum(moved + whole * leaving * state, axis=0, keepdims=True)
            totals.append(row_sum(everything))
            rq = scales[s, :, h : h + 1]
            rk = scales[s, :, heads + h : heads + h + 1]
            out = slice(h * 128, (h + 1) * 128)
            d_query = rq * (d_query - query * row_sum(query * d_query))
            d_key = rk * (d_key - key * row_sum(key * d_key))
            results[s, 1, :, out] = d_query.astype(jnp.bfloat16)
            results[s, 2, :, out] = d_key.astype(jnp.bfloat16)
            results[s, 3, :, out] = d_value.astype(jnp.bfloat16)
        packed = jnp.zeros((length, length), f32)
        for h in range(heads):
            packed = jnp.where(cols == h, columns[2 * h], packed)
            packed = jnp.where(cols == heads + h, columns[2 * h + 1], packed)
        turned = packed.T[: 2 * heads]
        decay_part = turned[:heads] - jnp.concatenate(column_rows, axis=0)
        decay_part = lax.dot_general(
            decay_part, suffix, (((1,), (0,)), ((), ())),
            preferred_element_type=f32, precision=lax.Precision.HIGHEST,
        ) + jnp.concatenate(totals, axis=0)
        grads[s] = jnp.concatenate([decay_part, turned[heads:]], axis=0) * slopes[s]
        return carry

    lax.fori_loop(0, devices, backward, 0)
    for mask, out in enumerate(sent):
        out[...] = results[flip(place[0], mask)]


PREPARE = 2


def call(kernel, name, scalars, outs, scratch=()):
    smem = pl.BlockSpec(memory_space=pltpu.SMEM)
    vmem = pl.BlockSpec(memory_space=pltpu.VMEM)

    def run(*operands):
        return pl.pallas_call(
            kernel,
            name=name,
            out_shape=outs,
            in_specs=[smem] * scalars + [vmem] * (len(operands) - scalars),
            out_specs=jax.tree.map(lambda _: vmem, outs),
            scratch_shapes=scratch,
        )(*operands)

    return run


def swapped(array, axis, mask):
    pairs = [(i, i ^ mask) for i in range(lax.axis_size(axis))]
    return lax.ppermute(array, axis, pairs)


def by_heads(
    hidden,
    query_in,
    key_in,
    value_in,
    w_proj,
    decay_rate,
    dt_bias,
    beta_bias,
    norm_gain,
    doc_starts,
    grad_out,
):
    f32, bf16 = jnp.float32, jnp.bfloat16
    devices, groups = lax.axis_size("ctx"), lax.axis_size("dp")
    place = lax.axis_index("ctx").astype(jnp.int32)
    group = lax.axis_index("dp").astype(jnp.int32)
    here, there = place.reshape(1), group.reshape(1)
    rows, width = hidden.shape[1:]
    depth = w_proj.shape[0]
    head_count = decay_rate.shape[0]
    heads = head_count // devices
    features = query_in.shape[2] // devices
    block_count = devices * rows // BLK

    turned = w_proj.T.reshape(2, devices, heads, depth).transpose(1, 0, 2, 3)
    turned = turned.reshape(2 * head_count, depth)
    weights = [turned] + [swapped(turned, "dp", m) for m in range(1, groups)]
    block = jax.ShapeDtypeStruct((4, rows, features), bf16)
    parts = call(pack_kernel, "pack", 1, [block] * devices)(
        here, query_in[0], key_in[0], value_in[0], grad_out[0]
    )
    received = [parts[0]] + [swapped(parts[m], "ctx", m) for m in range(1, devices)]

    logits = call(
        logits_kernel, "logits", 1, jax.ShapeDtypeStruct((2 * head_count, rows), f32)
    )(there, hidden[0], *weights)
    logits = lax.all_to_all(
        logits.reshape(devices, 2 * heads, rows), "ctx", 0, 0, tiled=True
    )

    def own(values):
        return lax.dynamic_slice_in_dim(values, place * heads, heads)[None, :, None]

    decay_in = logits[:, :heads] + own(dt_bias)
    beta = jax.nn.sigmoid(logits[:, heads:] + own(beta_bias))
    rate = own(decay_rate)
    log_decay = -rate * jax.nn.softplus(decay_in)
    upper = jnp.triu(jnp.ones((rows, rows), f32))
    cumulative = jnp.einsum("shi,ij->shj", log_decay, upper, precision=lax.Precision.HIGHEST)
    gate_rows = jnp.concatenate([cumulative, beta], axis=1)
    gate_cols = gate_rows.transpose(0, 2, 1)
    slopes = jnp.concatenate([-rate * jax.nn.sigmoid(decay_in), beta * (1.0 - beta)], axis=1)
    keep = keep_blocks(doc_starts[0], 0, block_count)

    scratch_block = pltpu.VMEM((devices, 4, rows, features), bf16)
    square = pltpu.VMEM((devices, heads, rows, rows), f32)
    outs = [block] * devices + [jax.ShapeDtypeStruct((devices, 2 * heads, rows), f32)]
    *results, grad_logits = call(
        functools.partial(core_kernel, heads, devices),
        "core",
        2,
        outs,
        [scratch_block, scratch_block]
        + [square] * 11
        + [
            pltpu.VMEM((devices, rows, 2 * heads), f32),
            pltpu.VMEM((heads, rows, rows), f32),
        ],
    )(here, keep, gate_rows, gate_cols, slopes, norm_gain.reshape(1, -1), *received)

    grad_logits = lax.all_to_all(grad_logits, "ctx", 0, 0, tiled=True)
    grad_logits = grad_logits.reshape(2 * head_count, rows)
    back, *terms = call(
        tail_kernel,
        "tail",
        1,
        [jax.ShapeDtypeStruct((rows, width), bf16)]
        + [jax.ShapeDtypeStruct((2 * head_count, depth), bf16)] * groups,
    )(there, hidden[0], grad_logits, *weights)
    total = terms[0].astype(f32)
    for m in range(1, groups):
        total = total + swapped(terms[m], "dp", m).astype(f32)
    bit = 1
    while bit < devices:
        total = total + swapped(total, "ctx", bit)
        bit *= 2
    total = total.reshape(devices, 2, heads, depth).transpose(1, 0, 2, 3)
    weight_grad = total.reshape(2 * head_count, depth).T

    returned = [results[0]] + [swapped(results[m], "ctx", m) for m in range(1, devices)]
    whole = jax.ShapeDtypeStruct((rows, query_in.shape[2]), bf16)
    normed, grad_q, grad_k, grad_v = call(unpack_kernel, "unpack", 1, [whole] * 4)(here, *returned)
    return (normed[None], grad_q[None], grad_k[None], grad_v[None], back[None], weight_grad)


def power_of_two(number):
    return number & (number - 1) == 0


def layer(*arrays):
    query, decay_rate, norm_gain = arrays[1], arrays[5], arrays[8]
    devices, groups = lax.axis_size("ctx"), lax.axis_size("dp")
    rows, head_count = query.shape[1], decay_rate.shape[0]
    fits = (
        power_of_two(devices)
        and power_of_two(groups)
        and head_count % devices == 0
        and rows == 2 * BLK == norm_gain.shape[0] == query.shape[2] // head_count
    )
    return by_heads(*arrays) if fits else shards(*arrays)


def solution(mesh):
    placed = (
        P("dp", "ctx", None),
        P("dp", "ctx", None),
        P("dp", "ctx", None),
        P("dp", "ctx", None),
        P("dp", None),
        P(),
        P(),
        P(),
        P(),
        P("dp", None),
        P("dp", "ctx", None),
    )
    return jax.shard_map(
        layer,
        mesh=mesh,
        in_specs=placed,
        out_specs=(
            P("dp", "ctx", None),
            P("dp", "ctx", None),
            P("dp", "ctx", None),
            P("dp", "ctx", None),
            P("dp", "ctx", None),
            P("dp", None),
        ),
        check_vma=False,
    )
```

```python
import functools

import jax
import jax.numpy as jnp
from jax import lax
from jax.experimental import pallas as pl
from jax.experimental.pallas import tpu as pltpu
from jax.sharding import PartitionSpec as P

BLK = 64


def entering(array, axis, combine, identity, reverse):
    devices, position = (lax.axis_size(axis), lax.axis_index(axis))
    everything = jax.tree.map(lambda part: lax.all_gather(part, axis), array)
    start = jax.tree.map(
        lambda part, zero: jnp.broadcast_to(jnp.asarray(zero, part.dtype), part.shape),
        array,
        identity,
    )

    def step(k, before):
        at = devices - 1 - k if reverse else k
        reached = at > position if reverse else at < position
        new = combine(before, jax.tree.map(lambda part: part[at], everything))
        return jax.tree.map(lambda a, b: jnp.where(reached, a, b), new, before)

    return lax.fori_loop(0, devices, step, start)


def unit_rows(matrix):
    return matrix * lax.rsqrt(jnp.sum(matrix * matrix, axis=-1, keepdims=True) + 1e-06)


def rms_scaled(values, norm_gain):
    return values * lax.rsqrt(jnp.mean(values * values, axis=-1, keepdims=True) + 1e-05) * norm_gain


def gate_terms(logit_rows, decay_rate, dt_bias, beta_bias):
    head_count = decay_rate.shape[0]
    log_decay = -decay_rate * jax.nn.softplus(logit_rows[:, :head_count] + dt_bias)
    beta_rows = jax.nn.sigmoid(logit_rows[:, head_count:] + beta_bias)
    return (log_decay, beta_rows)


def keep_blocks(starts, first_block, block_count):
    block_ids = first_block + jnp.arange(block_count, dtype=jnp.int32)
    starting = jnp.any(starts[:, None] == block_ids[None, :], axis=0) & (block_ids > 0)
    return jnp.where(starting, 0.0, 1.0).astype(jnp.float32)


def unit_lower_inverse(lower_matrix, length):
    maximum_precision = lax.Precision.HIGHEST
    identity_block = jnp.eye(length, dtype=jnp.float32)
    power_term = -lower_matrix
    inverse = identity_block + power_term
    squarings = max(1, (length - 1).bit_length())
    for level in range(squarings - 1):
        power_term = jnp.einsum("hij,hjk->hik", power_term, power_term, precision=maximum_precision)
        inverse = jnp.einsum(
            "hij,hjk->hik", inverse, identity_block + power_term, precision=maximum_precision
        )
    return inverse


def blockwise(query_rows, key_rows, value_rows, log_decay, beta_rows, keep_rows, state_first):
    head_count = log_decay.shape[-1]
    row_count = query_rows.shape[0]
    blocks = row_count // BLK
    key_dim = state_first.shape[1]
    state_width = state_first.shape[2]
    val_dim = value_rows.shape[1] // head_count
    maximum_precision = lax.Precision.HIGHEST

    def advance(state_now, pieces):
        query_piece, key_piece, value_piece, decay_piece, beta_piece, keep_piece = pieces
        length = query_piece.shape[0]
        query_unit = unit_rows(query_piece.astype(jnp.float32).reshape(length, head_count, key_dim))
        key_unit = unit_rows(key_piece.astype(jnp.float32).reshape(length, head_count, key_dim))
        value_heads = value_piece.astype(jnp.float32).reshape(length, head_count, val_dim)
        state_now = state_now * keep_piece
        cumulative = jnp.cumsum(decay_piece, axis=0).T
        spread = cumulative[:, :, None] - cumulative[:, None, :]
        row_ids = lax.broadcasted_iota(jnp.int32, (length, length), 0)
        col_ids = lax.broadcasted_iota(jnp.int32, (length, length), 1)
        lower_mask = row_ids >= col_ids
        strict_mask = row_ids > col_ids
        decay_ratio = jnp.where(lower_mask, jnp.exp(jnp.where(lower_mask, spread, 0.0)), 0.0)
        key_gram = jnp.einsum("ihd,jhd->hij", key_unit, key_unit, precision=maximum_precision)
        query_gram = jnp.einsum("ihd,jhd->hij", query_unit, key_unit, precision=maximum_precision)
        beta_heads = beta_piece.T
        lower_matrix = jnp.where(strict_mask, beta_heads[:, :, None] * key_gram * decay_ratio, 0.0)
        decay_now = jnp.exp(cumulative)
        right_side = jnp.concatenate(
            [
                beta_heads[:, :, None] * value_heads.transpose(1, 0, 2),
                (beta_heads * decay_now)[:, :, None] * key_unit.transpose(1, 0, 2),
            ],
            axis=-1,
        )
        inverse = unit_lower_inverse(lower_matrix, length)
        solved = jnp.einsum("hij,hjw->hiw", inverse, right_side, precision=maximum_precision)
        new_values = solved[..., :val_dim]
        key_weights = solved[..., val_dim:]
        new_values = jnp.concatenate(
            [new_values, jnp.zeros((head_count, length, state_width - val_dim), jnp.float32)],
            axis=-1,
        )
        corrected = new_values - jnp.einsum(
            "hcd,hdw->hcw", key_weights, state_now, precision=maximum_precision
        )
        from_state = jnp.einsum("chd,hdw->hcw", query_unit, state_now, precision=maximum_precision)
        output_piece = decay_now[:, :, None] * from_state + jnp.einsum(
            "hij,hjw->hiw", query_gram * decay_ratio, corrected, precision=maximum_precision
        )
        tail_decay = jnp.exp(cumulative[:, -1:] - cumulative)
        next_state = jnp.exp(cumulative[:, -1])[:, None, None] * state_now + jnp.einsum(
            "chd,hcw->hdw",
            key_unit,
            tail_decay[:, :, None] * corrected,
            precision=maximum_precision,
        )
        return (next_state, output_piece.transpose(1, 0, 2))

    final_state, outputs = lax.scan(
        advance,
        state_first,
        (
            query_rows.reshape(blocks, BLK, -1),
            key_rows.reshape(blocks, BLK, -1),
            value_rows.reshape(blocks, BLK, -1),
            log_decay.reshape(blocks, BLK, head_count),
            beta_rows.reshape(blocks, BLK, head_count),
            keep_rows,
        ),
    )
    return (outputs.reshape(row_count, head_count, state_width), final_state)


def combine_pairs(earlier_pair, later_pair):
    maximum_precision = lax.Precision.HIGHEST
    joined_map = jnp.einsum(
        "hij,hjk->hik", later_pair[0], earlier_pair[0], precision=maximum_precision
    )
    joined_offset = (
        jnp.einsum("hij,hjk->hik", later_pair[0], earlier_pair[1], precision=maximum_precision)
        + later_pair[1]
    )
    return (joined_map, joined_offset)


def shards(
    hidden,
    query_in,
    key_in,
    value_in,
    w_proj,
    decay_rate,
    dt_bias,
    beta_bias,
    norm_gain,
    doc_starts,
    grad_out,
):
    maximum_precision = lax.Precision.HIGHEST
    tokens_here = hidden[0]
    row_count = tokens_here.shape[0]
    head_count = decay_rate.shape[0]
    val_dim = norm_gain.shape[0]
    key_dim = query_in.shape[2] // head_count
    logits = jnp.dot(
        tokens_here,
        lax.all_gather(w_proj, "dp", axis=0, tiled=True),
        preferred_element_type=jnp.float32,
    )
    block_count = row_count // BLK
    keep_rows = keep_blocks(doc_starts[0], lax.axis_index("ctx") * block_count, block_count)
    identity_map = jnp.broadcast_to(
        jnp.eye(key_dim, dtype=jnp.float32), (head_count, key_dim, key_dim)
    )
    empty_state = jnp.zeros((head_count, key_dim, val_dim), jnp.float32)
    start_state = jnp.concatenate([empty_state, identity_map], axis=-1)

    def first_pass(query_rows, key_rows, value_rows, logit_rows):
        decay_part, beta_part = gate_terms(logit_rows, decay_rate, dt_bias, beta_bias)
        return blockwise(
            query_rows, key_rows, value_rows, decay_part, beta_part, keep_rows, start_state
        )

    pass_result, pull_core = jax.vjp(first_pass, query_in[0], key_in[0], value_in[0], logits)
    summary, closing = pass_result
    transfer = closing[..., val_dim:]
    offset = closing[..., :val_dim]
    state_sensitivity = summary[..., val_dim:]
    prefix = entering((transfer, offset), "ctx", combine_pairs, (identity_map, empty_state), False)
    incoming_state = prefix[1]
    mixed_rows = summary[..., :val_dim] + jnp.einsum(
        "ihd,hdl->ihl", state_sensitivity, incoming_state, precision=maximum_precision
    )
    normed_rows, pull_norm = jax.vjp(lambda values: rms_scaled(values, norm_gain), mixed_rows)
    incoming = grad_out[0].astype(jnp.float32).reshape(row_count, head_count, val_dim)
    mixed_gradient = pull_norm(incoming)[0]
    local_sensitivity = jnp.einsum(
        "idl,ids->dls", state_sensitivity, mixed_gradient, precision=maximum_precision
    )
    suffix = entering(
        (jnp.swapaxes(transfer, 1, 2), local_sensitivity),
        "ctx",
        combine_pairs,
        (identity_map, empty_state),
        True,
    )
    leaving = suffix[1]
    sensitivity_grad = jnp.einsum(
        "ihl,hdl->ihd", mixed_gradient, incoming_state, precision=maximum_precision
    )
    transfer_grad = jnp.einsum("hil,hjl->hij", leaving, incoming_state, precision=maximum_precision)
    summary_grad = jnp.concatenate([mixed_gradient, sensitivity_grad], axis=-1)
    closing_grad = jnp.concatenate([leaving, transfer_grad], axis=-1)
    grad_q, grad_k, grad_v, grad_logit = pull_core((summary_grad, closing_grad))
    rounded = grad_logit.astype(jnp.bfloat16)
    back_rows = jnp.dot(
        rounded,
        lax.all_gather(w_proj, "dp", axis=0, tiled=True).T,
        preferred_element_type=jnp.float32,
    )
    weight_term = lax.dot_general(
        tokens_here, rounded, (((0,), (0,)), ((), ())), preferred_element_type=jnp.float32
    )
    summed = lax.psum(weight_term, "ctx")
    weight_grad = lax.psum_scatter(summed, "dp", scatter_dimension=0, tiled=True)
    return (
        normed_rows.reshape(1, row_count, -1).astype(jnp.bfloat16),
        grad_q.reshape(1, row_count, -1),
        grad_k.reshape(1, row_count, -1),
        grad_v.reshape(1, row_count, -1),
        back_rows.astype(jnp.bfloat16).reshape(1, row_count, -1),
        weight_grad,
    )


def dot(a, b, ca, cb):
    return lax.dot_general(a, b, (((ca,), (cb,)), ((), ())), preferred_element_type=jnp.float32)


def halves(a):
    high = a.astype(jnp.bfloat16)
    return (high, (a - high.astype(jnp.float32)).astype(jnp.bfloat16))


def parts_of(a):
    return (a, None) if a.dtype == jnp.bfloat16 else halves(a)


def mul(a, b, ca=1, cb=0):
    ah, al = parts_of(a)
    bh, bl = parts_of(b)
    total = dot(ah, bh, ca, cb)
    if al is not None:
        total = total + dot(al, bh, ca, cb)
    if bl is not None:
        total = total + dot(ah, bl, ca, cb)
    return total


def one(a, b, ca=1, cb=0):
    return dot(a.astype(jnp.bfloat16), b.astype(jnp.bfloat16), ca, cb)


def row_sum(a):
    return jnp.sum(a, axis=1, keepdims=True)


def flip(index, mask):
    out = index
    bit = 1
    while bit <= mask:
        if mask & bit:
            out = out + bit * (1 - 2 * ((index // bit) % 2))
        bit *= 2
    return out


def pack_kernel(place, *refs):
    arrays, outs = refs[:4], refs[4:]
    width = outs[0].shape[2]
    for mask, out in enumerate(outs):
        at = pl.multiple_of(flip(place[0], mask) * width, width)
        for which, array in enumerate(arrays):
            out[which] = array[:, pl.ds(at, width)]


def unpack_kernel(place, *refs):
    outs = refs[-4:]
    for mask, part in enumerate(refs[:-4]):
        width = part.shape[2]
        at = pl.multiple_of(flip(place[0], mask) * width, width)
        for which, out in enumerate(outs):
            out[:, pl.ds(at, width)] = part[which]


def logits_kernel(place, hidden, *refs):
    out = refs[-1]
    total = None
    for mask, part in enumerate(refs[:-1]):
        depth = part.shape[1]
        at = pl.multiple_of(flip(place[0], mask) * depth, depth)
        term = dot(part[...], hidden[:, pl.ds(at, depth)], 1, 1)
        total = term if total is None else total + term
    out[...] = total


def tail_kernel(place, hidden, grads, *refs):
    count = (len(refs) - 1) // 2
    parts, back, outs = refs[:count], refs[count], refs[count + 1 :]
    rounded = grads[...].astype(jnp.bfloat16)
    for mask in range(count):
        depth = parts[mask].shape[1]
        at = pl.multiple_of(flip(place[0], mask) * depth, depth)
        back[:, pl.ds(at, depth)] = dot(rounded, parts[mask][...], 0, 0).astype(jnp.bfloat16)
        outs[mask][...] = dot(rounded, hidden[:, pl.ds(at, depth)], 1, 0).astype(outs[mask].dtype)


def head_part(pair, s, which, h, length):
    return pair[s, which, :, h * length : (h + 1) * length].astype(jnp.float32)


def decays(keep, gate_cols, s, h, heads):
    length = gate_cols.shape[1]
    second = lax.broadcasted_iota(jnp.int32, (length, 1), 0) >= length // 2
    column = gate_cols[s, :, h : h + 1]
    last = gate_cols[s, length - 1 :, h : h + 1]
    beta = gate_cols[s, :, heads + h : heads + h + 1]
    keep0, keep1 = keep[2 * s], keep[2 * s + 1]
    now = jnp.exp(column) * jnp.where(second, keep1, 1.0) * keep0
    tail = jnp.exp(last - column) * jnp.where(second, 1.0, keep1)
    whole = jnp.exp(last) * (keep0 * keep1)
    return (beta, now, tail, whole)


def grid_ids(length):
    rows = lax.broadcasted_iota(jnp.int32, (length, length), 0)
    cols = lax.broadcasted_iota(jnp.int32, (length, length), 1)
    return (rows, cols)


def ratio(keep, gate_rows, gate_cols, s, h):
    length = gate_cols.shape[1]
    rows, cols = grid_ids(length)
    same_half = (rows >= length // 2) == (cols >= length // 2)
    spread = gate_cols[s, :, h : h + 1] - gate_rows[s, h : h + 1, :]
    kept = jnp.where(same_half, 1.0, keep[2 * s + 1])
    return jnp.where(rows >= cols, jnp.exp(spread), 0.0) * kept


def each_group(devices, heads, size, body):
    size = min(size, devices)

    def step(at, carry):
        body([(at * size + k, h) for k in range(size) for h in range(heads)])
        return carry

    lax.fori_loop(0, devices // size, step, 0)


def in_step(parts):
    while parts:
        going = []
        for part in parts:
            try:
                next(part)
                going.append(part)
            except StopIteration:
                pass
        parts = going


def core_kernel(heads, devices, place, keep, gate_rows, gate_cols, slopes, gain, *refs):
    received, refs = (refs[:devices], refs[devices:])
    sent, refs = (refs[:devices], refs[devices:])
    grads, pair, results, qs, ks, ws, ps, xs, gs, ts, cs, states, leavings = refs[:13]
    us, bs, pulled, key_parts, betas, nows, tails, gammas, queries, keys, query_scales, key_scales = refs[13:25]
    row_parts = refs[25]
    length = gate_rows.shape[2]
    f32, bf16 = (jnp.float32, jnp.bfloat16)
    for mask, part in enumerate(received):
        pair[flip(place[0], mask)] = part[...]
    rows, cols = grid_ids(length)
    unit = jnp.where(rows == cols, 1.0, 0.0).astype(f32)
    gain_row = gain[...]
    ones = jnp.ones((2 * length, length), bf16)
    few_ones = jnp.ones((8, length), bf16)

    def wide_sum(values):
        return dot(jnp.concatenate(halves(values), axis=1), ones, 1, 0)

    def sum_row(values):
        high, low = halves(values)
        return (dot(few_ones, high, 1, 1) + dot(few_ones, low, 1, 1))[:1]

    def wide(column):
        return jnp.broadcast_to(column, (length, length))

    def prepare(items):
        work = []

        def one_prepare_1(s, h):
            query, key = (head_part(pair, s, 0, h, length), head_part(pair, s, 1, h, length))
            query_scale = lax.rsqrt(wide_sum(query * query) + 1e-06)
            yield
            key_scale = lax.rsqrt(wide_sum(key * key) + 1e-06)
            yield
            query_scales[s, h], key_scales[s, h] = (query_scale, key_scale)
            query, key = (query * query_scale, key * key_scale)
            queries[s, h], keys[s, h] = (query, key)
            qs[s, h], ks[s, h] = (query, key)
            beta, now, tail, _ = decays(keep, gate_cols, s, h, heads)
            betas[s, h], nows[s, h], tails[s, h] = (wide(beta), wide(now), wide(tail))
            gamma = ratio(keep, gate_rows, gate_cols, s, h)
            gammas[s, h] = gamma
            ps[s, h] = mul(query, key, 1, 1) * gamma
            yield
            gram = jnp.where(rows > cols, mul(key, key, 1, 1) * gamma, 0.0)
            yield
            gs[s, h] = gram.astype(bf16)
            work.append(betas[s, h] * gram)
        in_step([one_prepare_1(s, h) for s, h in items])
        found = [unit - jnp.where(rows // 2 == cols // 2, w, 0.0) for w in work]
        size = 2
        while size < length:
            joined = (rows // (2 * size) == cols // (2 * size)) & (rows // size != cols // size)
            inner = [one(jnp.where(joined, w, 0.0), x) for w, x in zip(work, found)]
            found = [x - mul(x, y) for x, y in zip(found, inner)]
            size *= 2

        def one_prepare_2(x, s, h):
            beta, now, tail = (betas[s, h], nows[s, h], tails[s, h])
            x = x - unit
            xs[s, h] = x
            weights = beta * now * keys[s, h]
            values = beta * head_part(pair, s, 2, h, length)
            weights = weights + mul(x, weights)
            yield
            values = values + mul(x, values)
            yield
            ws[s, h] = weights
            us[s, h] = values
            key = ks[s, h]
            ts[s, h] = mul(key, tail * weights, 0, 0).astype(bf16)
            yield
            bs[s, h] = mul(key, tail * values, 0, 0)
            yield
        in_step([one_prepare_2(x, s, h) for (s, h), x in zip(items, found)])
    each_group(devices, heads, PREPARE, prepare)
    running = [jnp.zeros((length, length), f32) for _ in range(heads)]
    for s in range(devices):
        for h in range(heads):
            states[s, h] = running[h]
            if s < devices - 1:
                whole = decays(keep, gate_cols, s, h, heads)[3]
                running[h] = whole * running[h] + bs[s, h] - mul(ts[s, h], running[h])

    def forward(items):

        def one_forward_3(s, h):
            now = nows[s, h]
            state, query, key, products = (states[s, h], qs[s, h], ks[s, h], ps[s, h])
            weights = ws[s, h]
            both = mul(jnp.concatenate([weights, query], axis=0), state, 1, 0)
            yield
            corrected = us[s, h] - both[:length]
            cs[s, h] = corrected.astype(bf16)
            from_state = now * both[length:]
            mixed = from_state + mul(products, corrected)
            yield
            scale = lax.rsqrt(wide_sum(mixed * mixed) * (1.0 / length) + 1e-05)
            yield
            out = slice(h * length, (h + 1) * length)
            results[s, 0, :, out] = (mixed * scale * gain_row).astype(bf16)
            slope = head_part(pair, s, 3, h, length) * gain_row
            inner = wide_sum(mixed * slope) * (1.0 / length)
            yield
            grad = scale * (slope - mixed * (scale * scale * inner))
            low_grad = grad
            back = mul(products, low_grad, 0, 0)
            yield
            pulled[s, h] = back
            scaled = now * grad
            bs[s, h] = mul(jnp.concatenate([query, weights], axis=0), jnp.concatenate([scaled, -back], axis=0), 0, 0)
            yield
            d_products = mul(low_grad, corrected, 1, 1)
            yield
            d_cross = d_products * gammas[s, h]
            d_query = mul(scaled, state, 1, 1) + mul(d_cross, key, 1, 0)
            yield
            key_parts[s, h] = mul(d_cross, query, 0, 0)
            yield
            terms = d_products * products.astype(f32)
            row_parts[s, h:h + 1, :] = sum_row(grad * from_state + terms) - jnp.sum(terms, axis=0, keepdims=True)
            yield
            query = queries[s, h]
            d_query = query_scales[s, h] * (d_query - query * wide_sum(query * d_query))
            yield
            results[s, 1, :, out] = d_query.astype(bf16)
        in_step([one_forward_3(s, h) for s, h in items])
    each_group(devices, heads, FORWARD, forward)
    suffix = jnp.where(rows >= cols, 1.0, 0.0).astype(f32)
    running = [jnp.zeros((length, length), f32) for _ in range(heads)]
    for s in reversed(range(devices)):
        for h in range(heads):
            leavings[s, h] = running[h].astype(bf16)
            if s > 0:
                whole = decays(keep, gate_cols, s, h, heads)[3]
                running[h] = whole * running[h] + bs[s, h] - mul(ts[s, h], running[h], 0, 0)

    def backward(items):
        decay_rows, beta_rows, totals = ([], [], [])

        def one_backward_4(s, h):
            whole = decays(keep, gate_cols, s, h, heads)[3]
            beta, now, tail = (betas[s, h], nows[s, h], tails[s, h])
            leaving, state, low_key, weights = (leavings[s, h], states[s, h], ks[s, h], ws[s, h])
            key = keys[s, h]
            key_leaving = mul(low_key, leaving, 1, 0)
            yield
            d_corr = pulled[s, h] + tail * key_leaving
            low_corr = d_corr.astype(bf16)
            d_weights = -mul(low_corr, state, 1, 1)
            yield
            tailed = tail * cs[s, h].astype(f32)
            d_key = key_parts[s, h] + one(tailed, leaving, 1, 1)
            yield
            d_solved = jnp.concatenate([d_corr, d_weights], axis=1)
            d_right = d_solved + one(xs[s, h], d_solved, 0, 0)
            yield
            d_right_u, d_right_w = (d_right[:, :length], d_right[:, length:])
            solved = jnp.concatenate([us[s, h], weights], axis=1)
            d_lower = jnp.where(rows > cols, -one(d_right, solved, 1, 1), 0.0)
            yield
            first_term = d_lower * gs[s, h].astype(f32)
            d_gram = beta * d_lower * gammas[s, h]
            d_key = d_key + one(d_gram + d_gram.T, low_key) + beta * now * d_right_w
            yield
            keyed = now * d_right_w * key
            moved = tailed * key_leaving
            scaled_term = beta * first_term
            kept = whole * leaving.astype(f32) * state.astype(f32)
            totals.append(row_sum(jnp.sum(moved + kept, axis=0, keepdims=True)))
            yield
            decay_rows.append(row_parts[s, h:h + 1, :] + sum_row(beta * keyed + scaled_term - moved) - jnp.sum(scaled_term, axis=0, keepdims=True))
            yield
            beta_rows.append(sum_row(d_right_u * head_part(pair, s, 2, h, length) + keyed + first_term))
            yield
            out = slice(h * length, (h + 1) * length)
            d_key = key_scales[s, h] * (d_key - key * wide_sum(key * d_key))
            yield
            results[s, 2, :, out] = d_key.astype(bf16)
            results[s, 3, :, out] = (beta * d_right_u).astype(bf16)
        in_step([one_backward_4(s, h) for s, h in items])
        rows_here = lax.dot_general(jnp.concatenate(decay_rows, axis=0), suffix, (((1,), (0,)), ((), ())), preferred_element_type=f32, precision=lax.Precision.HIGHEST) + jnp.concatenate(totals, axis=0)
        for at in range(0, len(items), heads):
            s = items[at][0]
            both = jnp.concatenate([rows_here[at:at + heads]] + beta_rows[at:at + heads], axis=0)
            grads[s] = both * slopes[s]
    each_group(devices, heads, BACKWARD, backward)
    for mask, out in enumerate(sent):
        out[...] = results[flip(place[0], mask)]


PREPARE, FORWARD, BACKWARD = 4, 4, 4


def call(kernel, name, scalars, outs, scratch=()):
    smem = pl.BlockSpec(memory_space=pltpu.SMEM)
    vmem = pl.BlockSpec(memory_space=pltpu.VMEM)

    def run(*operands):
        return pl.pallas_call(
            kernel,
            name=name,
            out_shape=outs,
            in_specs=[smem] * scalars + [vmem] * (len(operands) - scalars),
            out_specs=jax.tree.map(lambda _: vmem, outs),
            scratch_shapes=scratch,
        )(*operands)

    return run


def swapped(array, axis, mask):
    pairs = [(i, i ^ mask) for i in range(lax.axis_size(axis))]
    return lax.ppermute(array, axis, pairs)


def by_heads(
    hidden,
    query_in,
    key_in,
    value_in,
    w_proj,
    decay_rate,
    dt_bias,
    beta_bias,
    norm_gain,
    doc_starts,
    grad_out,
):
    f32, bf16 = jnp.float32, jnp.bfloat16
    devices, groups = lax.axis_size("ctx"), lax.axis_size("dp")
    place = lax.axis_index("ctx").astype(jnp.int32)
    group = lax.axis_index("dp").astype(jnp.int32)
    here, there = place.reshape(1), group.reshape(1)
    rows, width = hidden.shape[1:]
    depth = w_proj.shape[0]
    head_count = decay_rate.shape[0]
    heads = head_count // devices
    features = query_in.shape[2] // devices
    block_count = devices * rows // BLK

    turned = w_proj.T.reshape(2, devices, heads, depth).transpose(1, 0, 2, 3)
    turned = turned.reshape(2 * head_count, depth)
    weights = [turned] + [swapped(turned, "dp", m) for m in range(1, groups)]
    block = jax.ShapeDtypeStruct((4, rows, features), bf16)
    parts = call(pack_kernel, "pack", 1, [block] * devices)(
        here, query_in[0], key_in[0], value_in[0], grad_out[0]
    )
    received = [parts[0]] + [swapped(parts[m], "ctx", m) for m in range(1, devices)]

    logits = call(
        logits_kernel, "logits", 1, jax.ShapeDtypeStruct((2 * head_count, rows), f32)
    )(there, hidden[0], *weights)
    logits = lax.all_to_all(
        logits.reshape(devices, 2 * heads, rows), "ctx", 0, 0, tiled=True
    )

    def own(values):
        return lax.dynamic_slice_in_dim(values, place * heads, heads)[None, :, None]

    decay_in = logits[:, :heads] + own(dt_bias)
    beta = jax.nn.sigmoid(logits[:, heads:] + own(beta_bias))
    rate = own(decay_rate)
    log_decay = -rate * jax.nn.softplus(decay_in)
    upper = jnp.triu(jnp.ones((rows, rows), f32))
    cumulative = jnp.einsum("shi,ij->shj", log_decay, upper, precision=lax.Precision.HIGHEST)
    gate_rows = jnp.concatenate([cumulative, beta], axis=1)
    gate_cols = gate_rows.transpose(0, 2, 1)
    slopes = jnp.concatenate([-rate * jax.nn.sigmoid(decay_in), beta * (1.0 - beta)], axis=1)
    keep = keep_blocks(doc_starts[0], 0, block_count)

    scratch_block = pltpu.VMEM((devices, 4, rows, features), bf16)
    square = (devices, heads, rows, rows)
    outs = [block] * devices + [jax.ShapeDtypeStruct((devices, 2 * heads, rows), f32)]
    *results, grad_logits = call(
        functools.partial(core_kernel, heads, devices),
        "core",
        2,
        outs,
        [scratch_block, scratch_block]
        + [pltpu.VMEM(square, f32), pltpu.VMEM(square, f32), pltpu.VMEM(square, f32), pltpu.VMEM(square, f32), pltpu.VMEM(square, f32), pltpu.VMEM(square, bf16), pltpu.VMEM(square, bf16), pltpu.VMEM(square, bf16), pltpu.VMEM(square, f32), pltpu.VMEM(square, bf16)]
        + [pltpu.VMEM(square, f32)] * 12
        + [pltpu.VMEM((devices, heads, rows), f32)],
    )(here, keep, gate_rows, gate_cols, slopes, norm_gain.reshape(1, -1), *received)

    grad_logits = lax.all_to_all(grad_logits, "ctx", 0, 0, tiled=True)
    grad_logits = grad_logits.reshape(2 * head_count, rows)
    back, *terms = call(
        tail_kernel,
        "tail",
        1,
        [jax.ShapeDtypeStruct((rows, width), bf16)]
        + [jax.ShapeDtypeStruct((2 * head_count, depth), bf16)] * groups,
    )(there, hidden[0], grad_logits, *weights)
    total = terms[0].astype(f32)
    for m in range(1, groups):
        total = total + swapped(terms[m], "dp", m).astype(f32)
    bit = 1
    while bit < devices:
        total = total + swapped(total, "ctx", bit)
        bit *= 2
    total = total.reshape(devices, 2, heads, depth).transpose(1, 0, 2, 3)
    weight_grad = total.reshape(2 * head_count, depth).T

    returned = [results[0]] + [swapped(results[m], "ctx", m) for m in range(1, devices)]
    whole = jax.ShapeDtypeStruct((rows, query_in.shape[2]), bf16)
    normed, grad_q, grad_k, grad_v = call(unpack_kernel, "unpack", 1, [whole] * 4)(here, *returned)
    return (normed[None], grad_q[None], grad_k[None], grad_v[None], back[None], weight_grad)


def power_of_two(number):
    return number & (number - 1) == 0


def layer(*arrays):
    query, decay_rate, norm_gain = arrays[1], arrays[5], arrays[8]
    devices, groups = lax.axis_size("ctx"), lax.axis_size("dp")
    rows, head_count = query.shape[1], decay_rate.shape[0]
    fits = (
        power_of_two(devices)
        and power_of_two(groups)
        and head_count % devices == 0
        and rows == 2 * BLK == norm_gain.shape[0] == query.shape[2] // head_count
    )
    return by_heads(*arrays) if fits else shards(*arrays)


def solution(mesh):
    placed = (
        P("dp", "ctx", None),
        P("dp", "ctx", None),
        P("dp", "ctx", None),
        P("dp", "ctx", None),
        P("dp", None),
        P(),
        P(),
        P(),
        P(),
        P("dp", None),
        P("dp", "ctx", None),
    )
    return jax.shard_map(
        layer,
        mesh=mesh,
        in_specs=placed,
        out_specs=(
            P("dp", "ctx", None),
            P("dp", "ctx", None),
            P("dp", "ctx", None),
            P("dp", "ctx", None),
            P("dp", "ctx", None),
            P("dp", None),
        ),
        check_vma=False,
    )
```
